32 devices in a mesh: item: 8 (over z, y), code: 4 (over x, core).
Axes of the slice: x: 2, y: 2, z: 4, core: 2. Of those that a mesh axis runs over, the one named last changes fastest.
Arguments:
- residuals: float32 [256, 32768], P('code', 'item'), may hold values from -6 to 6
- codebook: float32 [256, 32768], P('item', 'code'), may hold values from -6 to 6
- item_weight: float32 [32768], P('item'), may hold values from 1 to 100
- code_capacity: float32 [32768], P('code'), may hold values from 0.25 to 4
- pairs: int32 [512, 64], P('item', 'code'), may hold values from -1 to 127, as said below
Outputs:
- item_potential: float32 [32768], P('item')
- code_potential: float32 [32768], P('code')
The draws below stay inside these ranges and needn't reach their ends.
Inputs may be any that keep to these rules, and one draw needn't show every extreme that they name: `pairs`: each entry is -1 (no candidate) or a code block's number within the code shard of its slot column. Within one item block and one code shard the live entries are distinct, the first slot is always live, and between 1 and 8 are live; some device holds exactly 8 live slots in every item block. Every code block is named by some item block.
All inputs are finite; a program needn't handle non-finite values.
Results may differ from the reference program's by a relative error of at most 0.0003.
Values sent between devices are 32-bit elements; how exact they have to be, the bound alone decides.
No kernel may reach another device: no remote copies, remote signals or barrier semaphores. Data moves between devices by JAX's collectives and lax.ppermute only.
A program may use at most 128 MiB of HBM per device.

```python
import math
import jax
import jax.numpy as jnp
from jax import lax

RESIDUAL_WIDTH = 256
BLOCK = 64
ITEM_DEV = 4096
CODE_DEV = 8192
SLOTS_DEV = 16
ITERS = 3
ITEMS = 32768
CODES = 32768
N_CODE = 4


def draw_pairs(key, part):
    item_blocks = ITEMS // BLOCK
    code_shards = CODES // CODE_DEV
    local_blocks = CODE_DEV // BLOCK
    half_slots = SLOTS_DEV // 2
    key_shift = jax.random.fold_in(key, 11)
    key_offset = jax.random.fold_in(key, 12)
    key_count = jax.random.fold_in(key, 13)
    key_heavy = jax.random.fold_in(key, 14)
    key_rank = jax.random.fold_in(key, 15)
    shift = jax.random.randint(key_shift, (1, code_shards), 0, local_blocks)
    base_ids = (jnp.arange(item_blocks, dtype=jnp.int32)[:, None] + shift) % local_blocks
    offset_keys = jax.random.split(key_offset, item_blocks * code_shards)
    offsets = jax.vmap(lambda one_key: jax.random.permutation(one_key, local_blocks - 1)[:SLOTS_DEV - 1])(offset_keys) + 1
    offsets = offsets.reshape(item_blocks, code_shards, SLOTS_DEV - 1).astype(jnp.int32)
    step_ids = jnp.concatenate([jnp.zeros((item_blocks, code_shards, 1), jnp.int32), offsets], axis=-1)
    block_ids = (base_ids[..., None] + step_ids) % local_blocks
    counts = jax.random.randint(key_count, (item_blocks, code_shards), 1, half_slots + 1)
    heavy_keys = jax.random.split(key_heavy, 2)
    heavy_item = jax.random.randint(heavy_keys[0], (), 0, ITEMS // ITEM_DEV)
    heavy_code = jax.random.randint(heavy_keys[1], (), 0, code_shards)
    block_shard = jnp.arange(item_blocks, dtype=jnp.int32) // (ITEM_DEV // BLOCK)
    heavy = (block_shard[:, None] == heavy_item) & (jnp.arange(code_shards, dtype=jnp.int32)[None, :] == heavy_code)
    counts = jnp.where(heavy, half_slots, counts)
    rank_keys = jax.random.split(key_rank, item_blocks * code_shards)
    ranks = jax.vmap(lambda one_key: jax.random.permutation(one_key, SLOTS_DEV - 1))(rank_keys)
    ranks = ranks.reshape(item_blocks, code_shards, SLOTS_DEV - 1)
    is_live = jnp.concatenate([jnp.ones((item_blocks, code_shards, 1), bool), ranks < (counts - 1)[..., None]], axis=-1)
    chosen = jnp.where(is_live, block_ids, -1)
    return chosen.reshape(item_blocks, code_shards * SLOTS_DEV).astype(jnp.int32)


def levels(rng, dims, shards, least, top_value):
    level, own = 1.0, jax.random.fold_in(rng, 6)
    for position, shards_of in shards:
        steps = jnp.exp(jax.random.uniform(jax.random.fold_in(own, position), (shards_of,), jnp.float32, least / len(shards), top_value / len(shards)))
        level = level * jnp.repeat(steps, dims[position] // shards_of).reshape([-1 if axis == position else 1 for axis in range(len(dims))])
    return level


def noise(own_key, shape, width, most, shards=(), kind=jnp.bfloat16):
    drawn = width * jax.random.normal(own_key, shape, jnp.float32)
    if shards:
        drawn = drawn * levels(own_key, shape, shards, -0.22, 0.18)
    return jnp.clip(drawn, -most, most).astype(kind)


def setup_inputs(seed: int = 0) -> dict:
    streams_of = jax.random.split(jax.random.key(seed), 6)
    residuals = noise(streams_of[0], (RESIDUAL_WIDTH, ITEMS), 1.0, 6.0, ((0, 4), (1, 8)), jnp.float32)
    codebook = noise(streams_of[1], (RESIDUAL_WIDTH, CODES), 1.0, 6.0, ((0, 8), (1, 4)), jnp.float32)
    item_weight = jnp.clip(jnp.exp(math.log(100.0) - 4.6051702 * jax.random.uniform(streams_of[2], (ITEMS,), jnp.float32) ** levels(streams_of[2], (ITEMS,), ((0, 8),), -0.2, 0.2)), 1.0, 100.0)
    code_capacity = jnp.clip(jnp.exp(math.log(4.0) - 2.7725887 * jax.random.uniform(streams_of[3], (CODES,), jnp.float32) ** levels(streams_of[3], (CODES,), ((0, 4),), -0.2, 0.2)), 0.25, 4.0)
    pairs = draw_pairs(jax.random.fold_in(streams_of[5], 71), 0)
    return {"residuals": residuals, "codebook": codebook, "item_weight": item_weight, "code_capacity": code_capacity, "pairs": pairs}


masked_score = -1e+30
softness_factor = 0.1

def reference(residuals, codebook, item_weight, code_capacity, pairs):
    item_blocks = ITEMS // BLOCK
    code_blocks = CODES // BLOCK
    local_blocks = CODE_DEV // BLOCK
    half_slots = SLOTS_DEV // 2
    logit_scale = 1.0 / (softness_factor * math.sqrt(RESIDUAL_WIDTH))
    item_logmass = jnp.log(item_weight) - jnp.log(jnp.sum(item_weight))
    code_logmass = jnp.log(code_capacity) - jnp.log(jnp.sum(code_capacity))
    logmass_blocks = item_logmass.reshape(item_blocks, BLOCK)
    grouped = pairs.reshape(item_blocks, N_CODE, SLOTS_DEV)
    order = jnp.argsort((grouped < 0).astype(jnp.int32), axis=2, stable=True)[:, :, :half_slots]
    packed = jnp.take_along_axis(grouped, order.astype(jnp.int32), axis=2)
    live_grouped = packed >= 0
    shard_base = (jnp.arange(N_CODE, dtype=jnp.int32) * local_blocks)[None, :, None]
    global_ids = jnp.where(live_grouped, packed + shard_base, 0).reshape(item_blocks, N_CODE * half_slots).astype(jnp.int32)
    is_live = live_grouped.reshape(item_blocks, N_CODE * half_slots)
    target = jnp.where(is_live, global_ids, code_blocks).astype(jnp.int32)
    catalogue_rows = residuals.T.reshape(item_blocks, BLOCK, RESIDUAL_WIDTH)
    code_rows = codebook.T.reshape(code_blocks, BLOCK, RESIDUAL_WIDTH)

    def tile_scores(block_index):
        picked = code_rows[global_ids[block_index]]
        scores = jnp.einsum('ir,sjr->sij', catalogue_rows[block_index], picked, precision=lax.Precision.HIGHEST) * logit_scale
        return jnp.where(is_live[block_index][:, None, None], scores, masked_score)
    block_range = jnp.arange(item_blocks, dtype=jnp.int32)
    code_potential = jnp.zeros((CODES,), jnp.float32)
    item_potential = jnp.zeros((ITEMS,), jnp.float32)
    for sweep in range(ITERS):
        code_split = code_potential.reshape(code_blocks, BLOCK)

        def block_pass(block_index):
            tiles = tile_scores(block_index)
            logits = tiles + code_split[global_ids[block_index]][:, None, :]
            row_peak = lax.optimization_barrier(jnp.max(logits, axis=(0, 2)))
            row_total = lax.optimization_barrier(jnp.sum(jnp.exp(logits - row_peak[None, :, None]), axis=(0, 2)))
            block_potential = logmass_blocks[block_index] - (row_peak + jnp.log(row_total))
            col_logits = tiles + block_potential[None, :, None]
            block_peak = lax.optimization_barrier(jnp.max(col_logits, axis=1))
            block_total = lax.optimization_barrier(jnp.sum(jnp.exp(col_logits - block_peak[:, None, :]), axis=1))
            live_row = is_live[block_index][:, None]
            return (block_potential, jnp.where(live_row, block_peak, masked_score), jnp.where(live_row, block_total, 0.0))
        potential_blocks, tile_peak, tile_total = lax.map(block_pass, block_range)
        item_potential = potential_blocks.reshape(ITEMS)
        flat_target = target.reshape(-1)
        peak_flat = tile_peak.reshape(-1, BLOCK)
        total_flat = tile_total.reshape(-1, BLOCK)
        col_peak = jnp.full((code_blocks + 1, BLOCK), masked_score, dtype=jnp.float32).at[flat_target].max(peak_flat)
        spread = total_flat * jnp.exp(peak_flat - col_peak[flat_target])
        col_total = jnp.zeros((code_blocks + 1, BLOCK), jnp.float32).at[flat_target].add(spread)
        col_lse = (col_peak[:code_blocks] + jnp.log(col_total[:code_blocks])).reshape(CODES)
        code_potential = code_logmass - col_lse
    return (item_potential, code_potential)
```

```python
import functools
import math

import jax
import jax.numpy as jnp
from jax import lax
from jax.experimental import pallas as pl
from jax.experimental.pallas import tpu as pltpu
from jax.sharding import PartitionSpec as P

BLOCK = 64
LANES = 128
EXTRA = 8
ITERS = 3

masked_score = -1e30
softness_factor = 0.1

AXES = ("item", "code")


class Grid:
    def __init__(self, items, codes):
        self.items, self.codes = items, codes
        self.R, self.X = items // 2, codes // 2
        assert self.R & (self.R - 1) == 0 and self.X & (self.X - 1) == 0

    def perm(self, target):
        pairs = []
        for r in range(self.R):
            for y in range(2):
                for x in range(self.X):
                    for c in range(2):
                        to = target(r, y, x, c)
                        if to is not None:
                            pairs.append((self.index(r, y, x, c), self.index(*to)))
        return pairs

    def index(self, r, y, x, c):
        return (2 * r + y) * self.codes + 2 * x + c

    def send(self, value, target):
        return lax.ppermute(value, AXES, self.perm(target))


def low_half(shape):
    return lax.broadcasted_iota(jnp.int32, shape, len(shape) - 1) < BLOCK


def flip(v):
    return pltpu.roll(v, BLOCK, 1)


def prep_kernel(n_pos, scale, *refs):
    ins, out = refs[: 2 * n_pos], refs[2 * n_pos]
    columns = out.shape[1] * BLOCK
    for pos in range(n_pos):
        for g in range(columns // LANES):
            at = pl.ds(g * LANES, LANES)
            v = jnp.concatenate([ins[2 * pos][:, at], ins[2 * pos + 1][:, at]], axis=0) * scale
            high = v.astype(jnp.bfloat16).astype(jnp.float32)
            both = jnp.concatenate([high, v - high], axis=0).T.astype(jnp.bfloat16)
            both = jnp.concatenate([both, both], axis=1)
            per = LANES // BLOCK
            out[pos, pl.ds(g * per, per)] = both.reshape(per, BLOCK, both.shape[1])


def prep_items(chunks, scale, n_blocks):
    n_pos = len(chunks)
    half = chunks[0][0].shape[0]
    depth = 8 * half
    step = 8
    ins = [h for pair in chunks for h in pair]
    return pl.pallas_call(
        functools.partial(prep_kernel, n_pos, scale),
        grid=(n_blocks // step,),
        in_specs=[pl.BlockSpec((half, step * BLOCK), lambda i: (0, i))] * len(ins),
        out_specs=pl.BlockSpec((n_pos, step, BLOCK, depth), lambda i: (0, i, 0, 0)),
        out_shape=jax.ShapeDtypeStruct((n_pos, n_blocks, BLOCK, depth), jnp.bfloat16),
        name="prep_items",
    )(*ins)


def row_stats(logits, b, n_blocks, stats):
    peak = functools.reduce(jnp.maximum, logits)
    peak = jnp.max(peak, axis=1, keepdims=True)
    total = functools.reduce(jnp.add, [jnp.exp(v - peak) for v in logits])
    total = jnp.sum(total, axis=1, keepdims=True)
    lane = lax.broadcasted_iota(jnp.int32, stats.shape, 1)
    return jnp.where(lane == b, peak, jnp.where(lane == n_blocks + b, total, stats))


def score_kernel(n_cand, first, last, n_blocks, sel, qtab, *refs):
    refs = list(refs)
    own = [refs.pop(0) for _ in range(n_cand)]
    partner = [refs.pop(0) for _ in range(n_cand)]
    x_ref, base_ref = refs.pop(0), refs.pop(0)
    capacity_ref = refs.pop(0) if last else None
    tile_ref = refs.pop(0)
    stats_ref = refs.pop(0) if last else None
    stage, w_ref, sem = refs
    h = own[0].shape[0]
    groups = stage.shape[1] // LANES
    gb = x_ref.shape[1]
    slots = tile_ref.shape[2] // BLOCK
    step = pl.program_id(0)

    @pl.when(step == 0)
    def _():
        c = sel[2]
        for n in range(n_cand):

            @pl.when(sel[0] == n)
            def _():
                a = pltpu.make_async_copy(own[n], stage.at[pl.ds(pl.multiple_of(c * h, h), h)], sem.at[0])
                d = pltpu.make_async_copy(
                    partner[n], stage.at[pl.ds(pl.multiple_of((1 - c) * h, h), h)], sem.at[1]
                )
                a.start()
                d.start()
                a.wait()
                d.wait()

        def convert(g, carry):
            v = stage[:, pl.ds(pl.multiple_of(g * LANES, LANES), LANES)]
            for j, u in enumerate((v, flip(v))):
                high = u.astype(jnp.bfloat16)
                low = (u - high.astype(jnp.float32)).astype(jnp.bfloat16)
                w_ref[j * groups + g] = jnp.concatenate([high, low], axis=0)
            return carry

        lax.fori_loop(0, groups, convert, 0, unroll=2)
        if last:
            stats_ref[...] = jnp.zeros_like(stats_ref)
            stats_ref[pl.ds(BLOCK, EXTRA), :] = jnp.full(
                (EXTRA, stats_ref.shape[1]), jnp.sum(capacity_ref[...]), jnp.float32
            )

    rows = w_ref.shape[1]
    lower = lax.broadcasted_iota(jnp.int32, (rows, LANES), 1) < BLOCK

    def one(j, stats):
        b = step * gb + j
        parts = []
        for k in range(slots // 2):
            w = jnp.where(lower, w_ref[qtab[b * slots + 2 * k]], w_ref[qtab[b * slots + 2 * k + 1]])
            high, low = w[: rows // 2], w[rows // 2 :]
            parts.append(jnp.concatenate([high, high, low, low], axis=0))
        scores = jnp.dot(x_ref[0, j], jnp.concatenate(parts, axis=1), preferred_element_type=jnp.float32)
        base = base_ref[pl.ds(j, 1), :] if first else base_ref[j]
        scores = scores + base
        tile_ref[j] = scores
        if last:
            logits = [scores[:, k * LANES : (k + 1) * LANES] for k in range(slots // 2)]
            stats = row_stats(logits, b, n_blocks, stats)
        return stats

    if last:
        body = pl.ds(0, BLOCK)
        stats_ref[body, :] = lax.fori_loop(0, gb, one, stats_ref[body, :], unroll=2)
    else:
        lax.fori_loop(0, gb, one, 0, unroll=2)


def score_pass(sel, qtab, own, partner, x, base, capacity, n_blocks, slots, first, last):
    gb = 8
    h, codes = own[0].shape
    width = slots * BLOCK
    tile = jax.ShapeDtypeStruct((n_blocks, BLOCK, width), jnp.float32)
    tile_spec = pl.BlockSpec((gb, BLOCK, width), lambda i, *_: (i, 0, 0))
    base_spec = pl.BlockSpec((gb, width), lambda i, *_: (i, 0)) if first else tile_spec
    args = [*own, *partner, x, base]
    in_specs = [pl.BlockSpec(memory_space=pl.ANY)] * (2 * len(own)) + [
        pl.BlockSpec((1, gb, BLOCK, x.shape[3]), lambda i, sel, q: (sel[1], i, 0, 0)),
        base_spec,
    ]
    out_shape, out_specs = [tile], [tile_spec]
    if last:
        args.append(capacity)
        in_specs.append(pl.BlockSpec(capacity.shape, lambda i, *_: (0, 0)))
        shape = (BLOCK + EXTRA, 2 * n_blocks)
        out_shape.append(jax.ShapeDtypeStruct(shape, jnp.float32))
        out_specs.append(pl.BlockSpec(shape, lambda i, *_: (0, 0)))
    return pl.pallas_call(
        functools.partial(score_kernel, len(own), first, last, n_blocks),
        grid_spec=pltpu.PrefetchScalarGridSpec(
            num_scalar_prefetch=2,
            grid=(n_blocks // gb,),
            in_specs=in_specs,
            out_specs=out_specs,
            scratch_shapes=[
                pltpu.VMEM((2 * h, codes), jnp.float32),
                pltpu.VMEM((2 * codes // LANES, 4 * h, LANES), jnp.bfloat16),
                pltpu.SemaphoreType.DMA((2,)),
            ],
        ),
        out_shape=out_shape,
        input_output_aliases={} if first else {2 + 2 * len(own) + 1: 0},
        name="score",
    )(sel, qtab, *args)


def row_kernel(n_blocks, sel, ptab, own_ref, other_ref, tile_ref, stats_ref, g_ref):
    gb = tile_ref.shape[0]
    slots = tile_ref.shape[2] // BLOCK
    half = own_ref.shape[0]
    step = pl.program_id(0)

    @pl.when(step == 0)
    def _():
        c = sel[2]
        g_ref[pl.ds(pl.multiple_of(c * half, 8), half), :] = own_ref[...]
        g_ref[pl.ds(pl.multiple_of((1 - c) * half, 8), half), :] = other_ref[...]
        g_ref[pl.ds(2 * half, EXTRA), :] = jnp.zeros((EXTRA, LANES), jnp.float32)
        stats_ref[...] = jnp.zeros_like(stats_ref)

    lower = low_half((1, LANES))

    def one(j, stats):
        b = step * gb + j
        logits = []
        for k in range(slots // 2):
            p0, p1 = ptab[b * slots + 2 * k], ptab[b * slots + 2 * k + 1]
            g = jnp.where(lower, g_ref[pl.ds(p0, 1), :], g_ref[pl.ds(p1, 1), :])
            logits.append(tile_ref[j, :, k * LANES : (k + 1) * LANES] + g)
        return row_stats(logits, b, n_blocks, stats)

    stats_ref[...] = lax.fori_loop(0, gb, one, stats_ref[...], unroll=2)


def row_pass(sel, ptab, g_own, g_other, tiles):
    gb = 8
    n_blocks, _, width = tiles.shape
    shape = (BLOCK, 2 * n_blocks)
    whole = lambda a: pl.BlockSpec(a.shape, lambda i, *_: (0, 0))
    return pl.pallas_call(
        functools.partial(row_kernel, n_blocks),
        grid_spec=pltpu.PrefetchScalarGridSpec(
            num_scalar_prefetch=2,
            grid=(n_blocks // gb,),
            in_specs=[
                whole(g_own),
                whole(g_other),
                pl.BlockSpec((gb, BLOCK, width), lambda i, *_: (i, 0, 0)),
            ],
            out_specs=pl.BlockSpec(shape, lambda i, *_: (0, 0)),
            scratch_shapes=[pltpu.VMEM((2 * g_own.shape[0] + EXTRA, LANES), jnp.float32)],
        ),
        out_shape=jax.ShapeDtypeStruct(shape, jnp.float32),
        name="row_pass",
    )(sel, ptab, g_own, g_other, tiles)


def col_kernel(n_stats, n_blocks, start, sel, ptab, *refs):
    refs = list(refs)
    stat_refs = [refs.pop(0) for _ in range(n_stats)]
    weight_ref, norm_ref, tile_ref = refs.pop(0), refs.pop(0), refs.pop(0)
    keep_ref, send_ref, f_ref, cap_ref = (refs.pop(0) for _ in range(4))
    peak_ref, total_ref = refs.pop(0), refs.pop(0)
    slots = tile_ref.shape[2] // BLOCK
    maxes, sums = refs[:slots], refs[slots:]
    gb = tile_ref.shape[0]
    step = pl.program_id(0)

    @pl.when(step == 0)
    def _():
        rows = [r[pl.ds(0, BLOCK), :] for r in stat_refs]
        m = functools.reduce(jnp.maximum, rows)
        t = functools.reduce(
            jnp.add, [pltpu.roll(a, a.shape[1] - n_blocks, 1) * jnp.exp(a - m) for a in rows]
        )
        lane = lax.broadcasted_iota(jnp.int32, m.shape, 1)
        valid = lane < n_blocks
        t = jnp.where(valid, t, 1.0)
        f = jnp.log(weight_ref[...]) - (m + jnp.log(t))
        if not start:
            f = f - norm_ref[0:1, :]
        f_ref[...] = jnp.where(valid, f, 0.0)
        if start:
            caps = functools.reduce(jnp.add, [r[pl.ds(BLOCK, EXTRA), :] for r in stat_refs])
            cap_ref[...] = jnp.log(caps)
        else:
            cap_ref[...] = jnp.zeros_like(cap_ref)
        for s in range(slots):
            maxes[s][...] = jnp.full(maxes[s].shape, masked_score, jnp.float32)
            sums[s][...] = jnp.zeros(sums[s].shape, jnp.float32)

    f_all = f_ref[...]
    lane_f = lax.broadcasted_iota(jnp.int32, f_all.shape, 1)

    def one(j, carry):
        b = step * gb + j
        f = jnp.sum(jnp.where(lane_f == b, f_all, 0.0), axis=1, keepdims=True)
        for k in range(slots // 2):
            at = slice(k * LANES, (k + 1) * LANES)
            logits = tile_ref[j, :, at] + f
            peak = jnp.max(logits, axis=0, keepdims=True)
            total = jnp.sum(jnp.exp(logits - peak), axis=0, keepdims=True)
            peak_ref[k, pl.ds(b, 1), :] = peak
            total_ref[k, pl.ds(b, 1), :] = total
            for s in (2 * k, 2 * k + 1):
                row = pl.ds(ptab[b * slots + s], 1)
                maxes[s][row, :] = jnp.maximum(maxes[s][row, :], peak)
        return carry

    lax.fori_loop(0, gb, one, 0, unroll=2)

    @pl.when(step == pl.num_programs(0) - 1)
    def _():
        lower = low_half(maxes[0].shape)

        def joined(parts, op):
            even = functools.reduce(op, [parts[s][...] for s in range(0, slots, 2)])
            odd = functools.reduce(op, [parts[s][...] for s in range(1, slots, 2)])
            return jnp.where(lower, op(even, flip(odd)), op(odd, flip(even)))

        top = joined(maxes, jnp.maximum)
        maxes[0][...] = top
        lower_row = low_half((1, LANES))

        def spread(b, carry):
            for k in range(slots // 2):
                p0, p1 = ptab[b * slots + 2 * k], ptab[b * slots + 2 * k + 1]
                peak = jnp.where(lower_row, maxes[0][pl.ds(p0, 1), :], maxes[0][pl.ds(p1, 1), :])
                part = total_ref[k, pl.ds(b, 1), :] * jnp.exp(peak_ref[k, pl.ds(b, 1), :] - peak)
                for s, p in ((2 * k, p0), (2 * k + 1, p1)):
                    sums[s][pl.ds(p, 1), :] += part
            return carry

        lax.fori_loop(0, n_blocks, spread, 0, unroll=4)
        maxes[1][...] = jnp.where(lower, top, joined(sums, jnp.add))
        c = sel[2]
        half = keep_ref.shape[0] - EXTRA
        body, tail = pl.ds(0, half), pl.ds(half, EXTRA)
        keep_ref[body, :] = maxes[1][pl.ds(pl.multiple_of(c * half, 8), half), :]
        send_ref[body, :] = maxes[1][pl.ds(pl.multiple_of((1 - c) * half, 8), half), :]
        weights = jnp.where(lane_f < n_blocks, weight_ref[...], 0.0)
        weights = jnp.full((EXTRA, LANES), jnp.sum(weights), jnp.float32)
        keep_ref[tail, :] = weights
        send_ref[tail, :] = weights


def col_pass(sel, ptab, stats, weights, norm, tiles, code_blocks, start):
    gb = 8
    n_blocks, _, width = tiles.shape
    slots = width // BLOCK
    whole = lambda a: pl.BlockSpec(a.shape, lambda i, *_: (0, 0))
    half = jax.ShapeDtypeStruct((code_blocks // 2 + EXTRA, LANES), jnp.float32)
    outs = [
        half,
        half,
        jax.ShapeDtypeStruct(weights.shape, jnp.float32),
        jax.ShapeDtypeStruct((EXTRA, stats[0].shape[1]), jnp.float32),
    ]
    return pl.pallas_call(
        functools.partial(col_kernel, len(stats), n_blocks, start),
        grid_spec=pltpu.PrefetchScalarGridSpec(
            num_scalar_prefetch=2,
            grid=(n_blocks // gb,),
            in_specs=[whole(a) for a in (*stats, weights, norm)]
            + [pl.BlockSpec((gb, BLOCK, width), lambda i, *_: (i, 0, 0))],
            out_specs=[whole(a) for a in outs],
            scratch_shapes=[pltpu.VMEM((slots // 2, n_blocks, LANES), jnp.float32)] * 2
            + [pltpu.VMEM((code_blocks + EXTRA, LANES), jnp.float32)] * (2 * slots),
        ),
        out_shape=outs,
        name="col_pass",
    )(sel, ptab, *stats, weights, norm, tiles)


def merge(parts):
    lower = low_half(parts[0].shape)
    flips = [flip(a) for a in parts]
    peaks = [jnp.where(lower, a, b) for a, b in zip(parts, flips)]
    totals = [jnp.where(lower, b, a) for a, b in zip(parts, flips)]
    peak = functools.reduce(jnp.maximum, peaks)
    total = functools.reduce(jnp.add, [t * jnp.exp(p - peak) for p, t in zip(peaks, totals)])
    return peak, total


def join_kernel(a_ref, b_ref, out_ref):
    half = out_ref.shape[0] - EXTRA
    body, tail = pl.ds(0, half), pl.ds(half, EXTRA)
    peak, total = merge([a_ref[body, :], b_ref[body, :]])
    out_ref[body, :] = jnp.where(low_half(peak.shape), peak, total)
    out_ref[tail, :] = a_ref[tail, :] + b_ref[tail, :]


def join(a, b):
    return pl.pallas_call(join_kernel, out_shape=jax.ShapeDtypeStruct(a.shape, jnp.float32), name="join")(a, b)


def finish_kernel(n, start, sel, *refs):
    parts = refs[:n]
    capacity_ref, cap_ref, g_ref, norm_ref = refs[n:]
    half = g_ref.shape[0]
    body, tail = pl.ds(0, half), pl.ds(half, EXTRA)
    peak, total = merge([r[body, :] for r in parts])
    capacity = capacity_ref[pl.ds(pl.multiple_of(sel[2] * half, 8), half), :]
    g = jnp.log(capacity) - cap_ref[0:1, 0:LANES] - (peak + jnp.log(total))
    norm = jnp.log(functools.reduce(jnp.add, [r[tail, :] for r in parts]))
    norm_ref[...] = norm
    g_ref[...] = g + norm[0:1, :] if start else g


def finish(sel, parts, capacity, cap, start):
    half = capacity.shape[0] // 2
    whole = pl.BlockSpec(memory_space=pltpu.VMEM)
    return pl.pallas_call(
        functools.partial(finish_kernel, len(parts), start),
        in_specs=[pl.BlockSpec(memory_space=pltpu.SMEM)] + [whole] * (len(parts) + 2),
        out_specs=[whole, whole],
        out_shape=[
            jax.ShapeDtypeStruct((half, LANES), jnp.float32),
            jax.ShapeDtypeStruct((EXTRA, LANES), jnp.float32),
        ],
        name="finish",
    )(sel, *parts, capacity, cap)


def compact(pairs, slots, code_blocks):
    live = pairs >= 0
    rank = jnp.cumsum(live.astype(jnp.int32), axis=1) - 1
    hit = live[:, :, None] & (rank[:, :, None] == jnp.arange(slots, dtype=jnp.int32))
    return code_blocks + jnp.sum(jnp.where(hit, pairs[:, :, None] - code_blocks, 0), axis=1)


def body(grid, residuals, codebook, item_weight, code_capacity, pairs):
    R, X = grid.R, grid.X
    r, y = lax.axis_index("item") // 2, lax.axis_index("item") % 2
    x, c = lax.axis_index("code") // 2, lax.axis_index("code") % 2
    width = residuals.shape[0] * grid.codes
    n_items, n_codes = residuals.shape[1], codebook.shape[1]
    n_blocks, code_blocks = n_items // BLOCK, n_codes // BLOCK
    slots = pairs.shape[1] // 2
    scale = 1.0 / (softness_factor * math.sqrt(width))
    swapped = lambda r, y, x, c: (r, c, x, y)
    to_core = lambda r, y, x, c: (r, y, x, 1 - c)
    to_y = lambda r, y, x, c: (r, 1 - y, x, c)

    codes = grid.send(codebook, swapped)
    small = jnp.concatenate(
        [
            pairs.astype(jnp.float32).reshape(-1),
            item_weight,
            code_capacity,
        ]
    ).reshape(-1, LANES)
    small = grid.send(small, swapped).reshape(-1)
    n_pairs = pairs.size
    pairs = small[:n_pairs].reshape(pairs.shape).astype(jnp.int32)
    weights = small[n_pairs : n_pairs + n_items].reshape(n_blocks, BLOCK).T
    weights = jnp.concatenate([weights, jnp.ones_like(weights)], axis=1)
    capacity = small[n_pairs + n_items :].reshape(code_blocks, BLOCK)
    capacity_sum = capacity.reshape(-1, LANES)
    capacity = jnp.concatenate([capacity, capacity], axis=1)

    residuals, codes = lax.optimization_barrier((residuals, codes))
    ups, downs = {0: codes}, {0: codes}
    for s in range(1, R):
        ups[s] = grid.send(ups[s - 1], lambda r, y, x, c: (r + 1, y, x, c) if s - 1 <= r < R - 1 else None)
        downs[s] = grid.send(downs[s - 1], lambda r, y, x, c: (r - 1, y, x, c) if 0 < r <= R - s else None)
    up_partner = {0: grid.send(codes, to_core)}
    down_partner = {0: up_partner[0]}
    for s in range(1, R):
        up_partner[s] = grid.send(ups[s], lambda r, y, x, c: (r, y, x, 1 - c) if r >= s else None)
        down_partner[s] = grid.send(downs[s], lambda r, y, x, c: (r, y, x, 1 - c) if r < R - s else None)

    items = grid.send(residuals, swapped)
    halves = lambda v: (v[: v.shape[0] // 2], v[v.shape[0] // 2 :])
    from_y = grid.send(items, to_y)
    chunks = [halves(items), halves(from_y)]
    for m in range(1, X):
        to_x = lambda r, y, x, c: (r, y, x ^ m, c)
        from_x = grid.send(items, to_x)
        chunks.append(halves(from_x))
        chunks.append((grid.send(chunks[1][0], to_x), grid.send(halves(from_x)[1], to_y)))
    x_all = prep_items(chunks, scale, n_blocks)

    ids = compact(pairs, slots, code_blocks)
    live = ids < code_blocks
    ptab = ids.reshape(-1)
    safe = jnp.where(live, ids, 0)
    parity = (safe + jnp.arange(slots, dtype=jnp.int32)) % 2
    qtab = (parity * (code_blocks // 2) + safe // 2).reshape(-1)
    penalty = jnp.repeat(jnp.where(live, 0.0, masked_score).astype(jnp.float32), BLOCK, axis=1)

    order = []
    for me in range(R):
        arrivals = [(s, side, me - s if side == 0 else me + s) for s in range(1, R) for side in (0, 1)]
        order.append([(0, 0, me)] + [a for a in arrivals if 0 <= a[2] < R])
    tiles, stats = penalty, None
    for n in range(R):
        cands = sorted({o[n][:2] for o in order})
        pick = jnp.array([cands.index(o[n][:2]) for o in order], jnp.int32)[r]
        source = jnp.array([o[n][2] for o in order], jnp.int32)[r]
        sel = jnp.stack([pick, source ^ (2 * x + y), c, c]).astype(jnp.int32)
        own = [(ups, downs)[side][s] for s, side in cands]
        partner = [(up_partner, down_partner)[side][s] for s, side in cands]
        out = score_pass(
            sel, qtab, own, partner, x_all, tiles, capacity_sum, n_blocks, slots, n == 0, n == R - 1
        )
        tiles = out[0]
    stats = out[1]

    norm = jnp.zeros((EXTRA, LANES), jnp.float32)
    cap = None
    for sweep in range(ITERS):
        start = sweep == 0
        parts = [stats]
        for m in range(1, 2 * X):
            parts.append(grid.send(stats, lambda r, y, x, c: (r, y ^ (m & 1), x ^ (m >> 1), c)))
        keep, give, f, new_cap = col_pass(sel, ptab, parts, weights, norm, tiles, code_blocks, start)
        cap = new_cap if start else cap
        mine = join(keep, grid.send(give, to_core))
        parts = [mine]
        for m in range(1, R):
            parts.append(grid.send(mine, lambda r, y, x, c: (r ^ m, y, x, c)))
        g, new_norm = finish(sel, parts, capacity, cap, start)
        norm = new_norm if start else norm
        if sweep < ITERS - 1:
            stats = row_pass(sel, ptab, g, grid.send(g, to_core), tiles)

    item_potential = grid.send(f[:, :n_blocks].T.reshape(n_items), swapped)
    g = g[:, :BLOCK]
    near = grid.send(g, swapped)
    far = grid.send(g, lambda r, y, x, c: (r, 1 - c, x, y))
    code_potential = jnp.where(y == 0, jnp.concatenate([near, far]), jnp.concatenate([far, near]))
    return item_potential, code_potential.reshape(n_codes)


def solution(mesh):
    placed = (P("code", "item"), P("item", "code"), P("item"), P("code"), P("item", "code"))
    grid = Grid(mesh.shape["item"], mesh.shape["code"])
    return jax.shard_map(
        functools.partial(body, grid),
        mesh=mesh,
        in_specs=placed,
        out_specs=(P("item"), P("code")),
        check_vma=False,
    )
```
